32 devices in a mesh: dp: 8 (over z, core), expert: 4 (over y, x).
Axes of the slice: x: 2, y: 2, z: 4, core: 2. Of those that a mesh axis runs over, the one named last changes fastest.
Arguments:
- tokens: bfloat16 [24576, 2048], P(('dp', 'expert')), may hold values from -6 to 6
- target: bfloat16 [24576, 2048], P(('dp', 'expert')), may hold values from -4 to 4
- route_index: int32 [8, 4, 4, 16], P('dp', None, 'expert'), may hold values from 0 to 767, as said below
- route_count: int32 [8, 4, 4], P('dp', None, 'expert'), may hold values from 1 to 16, as said below
- route_gate: float32 [8, 4, 4, 16], P('dp', None, 'expert'), may hold values from 0.1 to 1
- gate_weight: bfloat16 [2048, 4, 768], P('dp', 'expert'), may hold values from -0.125 to 0.125
- up_weight: bfloat16 [2048, 4, 768], P('dp', 'expert'), may hold values from -0.125 to 0.125
- down_weight: bfloat16 [2048, 4, 768], P('dp', 'expert'), may hold values from -0.21875 to 0.21875
Outputs:
- token_grad: bfloat16 [24576, 2048], P(('dp', 'expert'))
- gate_gradient: float32 [2048, 4, 768], P('dp', 'expert')
- up_gradient: float32 [2048, 4, 768], P('dp', 'expert')
- down_gradient: float32 [2048, 4, 768], P('dp', 'expert')
The draws below stay inside these ranges and needn't reach their ends.
Inputs may be any that keep to these rules, and one draw needn't show every extreme that they name: `route_index`: within each list of 16 slots the indices are distinct; each names a token of the source device. `route_count`: in every group one expert has all 16 slots live from every source device; slots at or beyond the count are unused.
All inputs are finite; a program needn't handle non-finite values.
Results may differ from the reference program's by a relative error of at most 0.0059.
Values may be sent and summed in bfloat16 or wider, within the bound.
A program may use at most 128 MiB of HBM per device.

```python
import jax
import jax.numpy as jnp

D = 2048
FF = 768
TOK_DEV = 768
SLOTS = 16
GROUPS = 8
SOURCES = 4
EXPERTS = 4
TOKENS = 24576


def draw_route_count(key, part):
    keys_all = jax.random.split(jax.random.fold_in(key, 11), 3)
    shift_by = jax.random.randint(keys_all[0], (GROUPS, EXPERTS, 1), 0, 4).astype(jnp.int32)
    level_top = jnp.maximum(jnp.right_shift(jnp.full((GROUPS, EXPERTS, 1), SLOTS, jnp.int32), shift_by), 1)
    level_low = jnp.maximum(level_top // 2, 1)
    counts_drawn = jax.random.randint(keys_all[1], (GROUPS, EXPERTS, SOURCES), level_low, level_top + 1)
    full_expert = jax.random.randint(keys_all[2], (GROUPS, 1, 1), 0, EXPERTS)
    filled = jnp.where(jnp.arange(EXPERTS, dtype=jnp.int32)[None, :, None] == full_expert, SLOTS, counts_drawn)
    return filled.astype(jnp.int32)


def draw_route_index(key, part):
    keys_all = jax.random.split(jax.random.fold_in(key, 23), GROUPS * EXPERTS * SOURCES)
    chosen = jax.vmap(lambda subkey: jax.random.permutation(subkey, TOK_DEV)[:SLOTS])(keys_all)
    return chosen.reshape(GROUPS, EXPERTS, SOURCES, SLOTS).astype(jnp.int32)


def block_scale(own_key, dims, pieces, smallest, top_value):
    level = 1.0
    for position, parts in pieces:
        heights = jax.random.uniform(jax.random.fold_in(jax.random.fold_in(own_key, 6), position), (parts,), jnp.float32, smallest / len(pieces), top_value / len(pieces))
        level = level * jnp.repeat(jnp.exp(heights), dims[position] // parts).reshape((-1,) + (1,) * (len(dims) - 1 - position))
    return level


def scatter_about(own_key, shape, deviation, most, shards=(), held_as=jnp.bfloat16):
    gain = block_scale(own_key, shape, shards, -0.22, 0.18) if shards else 1.0
    array = jax.random.normal(own_key, shape, jnp.float32) * deviation * gain
    return jnp.minimum(jnp.maximum(array, -most), most).astype(held_as)


def setup_inputs(seed: int = 0) -> dict:
    splits = jax.random.split(jax.random.key(seed), 9)
    tokens = scatter_about(splits[0], (TOKENS, D), 1.0, 6.0, ((0, 32),))
    target = scatter_about(splits[1], (TOKENS, D), 0.5, 4.0, ((0, 32),))
    route_index = draw_route_index(jax.random.fold_in(splits[8], 71), 0)
    route_count = draw_route_count(jax.random.fold_in(splits[8], 71), 0)
    route_gate = jnp.clip(0.1 + 0.9 * jax.random.uniform(splits[4], (GROUPS, EXPERTS, SOURCES, SLOTS), jnp.float32) ** block_scale(splits[4], (GROUPS, EXPERTS, SOURCES, SLOTS), ((0, 8), (2, 4)), -0.2, 0.2), 0.1, 1.0)
    gate_weight = scatter_about(splits[5], (D, EXPERTS, FF), D ** -0.5, 0.125, ((0, 8), (1, 4)))
    up_weight = scatter_about(splits[6], (D, EXPERTS, FF), D ** -0.5, 0.125, ((0, 8), (1, 4)))
    down_weight = scatter_about(splits[7], (D, EXPERTS, FF), FF ** -0.5, 0.21875, ((0, 8), (1, 4)))
    return {"tokens": tokens, "target": target, "route_index": route_index, "route_count": route_count, "route_gate": route_gate, "gate_weight": gate_weight, "up_weight": up_weight, "down_weight": down_weight}


def reference(tokens, target, route_index, route_count, route_gate, gate_weight, up_weight, down_weight):
    groups, experts, sources, per_source = route_index.shape
    model_width = tokens.shape[1]
    device_tokens = tokens.shape[0] // (groups * sources)
    usable = jnp.arange(per_source, dtype=jnp.int32)[None, None, None, :] < route_count[:, :, :, None]
    offsets = (jnp.arange(groups, dtype=jnp.int32)[:, None, None, None] * sources + jnp.arange(sources, dtype=jnp.int32)[None, None, :, None]) * device_tokens
    slot_token = (offsets + route_index).astype(jnp.int32).reshape(groups, experts, sources * per_source)
    slot_weight = jnp.where(usable, route_gate, 0.0).astype(jnp.float32).reshape(groups, experts, sources * per_source)
    usable_rows = usable.reshape(groups, experts, sources * per_source)
    expert_rows = tokens[slot_token] * usable_rows[..., None].astype(tokens.dtype)
    rows_wide = expert_rows.astype(jnp.float32)
    gate_wide = gate_weight.astype(jnp.float32)
    up_wide = up_weight.astype(jnp.float32)
    down_wide = down_weight.astype(jnp.float32)
    gate_pre = jnp.einsum("gerd,def->gerf", rows_wide, gate_wide)
    up_pre = jnp.einsum("gerd,def->gerf", rows_wide, up_wide)
    sigma = jax.nn.sigmoid(gate_pre)
    active = gate_pre * sigma
    hidden = (active * up_pre).astype(jnp.bfloat16)
    expert_out = jnp.einsum("gerf,def->gerd", hidden.astype(jnp.float32), down_wide).astype(jnp.bfloat16)
    flat_token = slot_token.reshape(-1)
    combined = jnp.zeros((tokens.shape[0], model_width), jnp.float32).at[flat_token].add(
        (slot_weight[..., None] * expert_out.astype(jnp.float32)).reshape(-1, model_width))
    out_grad = combined - target.astype(jnp.float32)
    slot_grad = (slot_weight[..., None] * out_grad[slot_token]).astype(jnp.bfloat16)
    hidden_grad = jnp.einsum("gerd,def->gerf", slot_grad.astype(jnp.float32), down_wide)
    gate_grad = (hidden_grad * up_pre * sigma * (1.0 + gate_pre * (1.0 - sigma))).astype(jnp.bfloat16)
    up_grad = (hidden_grad * active).astype(jnp.bfloat16)
    row_grad = (jnp.einsum("gerf,def->gerd", gate_grad.astype(jnp.float32), gate_wide)
                + jnp.einsum("gerf,def->gerd", up_grad.astype(jnp.float32), up_wide)).astype(jnp.bfloat16)
    token_grad = jnp.zeros((tokens.shape[0], model_width), jnp.float32).at[flat_token].add(
        row_grad.astype(jnp.float32).reshape(-1, model_width)).astype(jnp.bfloat16)
    factor = (groups * sources * per_source) ** -0.5
    gate_gradient = jnp.einsum("gerd,gerf->def", rows_wide, gate_grad.astype(jnp.float32)) * factor
    up_gradient = jnp.einsum("gerd,gerf->def", rows_wide, up_grad.astype(jnp.float32)) * factor
    down_gradient = jnp.einsum("gerd,gerf->def", slot_grad.astype(jnp.float32), hidden.astype(jnp.float32)) * factor
    return token_grad, gate_gradient, up_gradient, down_gradient
```

```python
import functools

import jax
import jax.numpy as jnp
from jax import lax
from jax.experimental import pallas as pl
from jax.experimental.pallas import tpu as pltpu
from jax.sharding import PartitionSpec as P

F32 = jnp.float32
BF16 = jnp.bfloat16
CORES = 2


def dot(a, b, dims, precision=None):
    return lax.dot_general(
        a, b, (dims, ((), ())), preferred_element_type=F32, precision=precision
    )


NN = ((1,), (0,))
NT = ((1,), (1,))
TN = ((0,), (0,))


def kernel(
    planes, experts, slots, factor,
    rows, tgt, amat, wcol, gw, uw, dw,
    cb_out, gg_out, ug_out, dg_out,
    W, R, EO, RET, SG, G, RG, CB, PS, PR, HS, HR, H, GU, RX, GX, HX, GUX,
    w_loc, w_send, w_recv, a_loc, a_send, a_recv, p_send, p_recv,
    h_send, h_recv, x_send, x_recv,
):
    dp = lax.axis_index("dp")
    me_e = lax.axis_index("expert")
    me_z = dp // CORES
    core = dp % CORES
    peers = planes * experts
    per_group = experts * slots
    all_rows = planes * per_group
    half = gw.shape[0]
    chunk = CORES * half
    ff = gw.shape[1]
    me = me_z * experts + me_e
    sibling = {"dp": me_z * CORES + (1 - core), "expert": me_e}

    def at(z, e):
        return {"dp": z * CORES + core, "expert": e}

    barrier = pltpu.get_barrier_semaphore()

    def greet(k, carry):
        p = (me + k) % peers
        pl.semaphore_signal(
            barrier, inc=1, device_id=at(p // experts, p % experts),
            device_id_type=pl.DeviceIdType.MESH,
        )
        return carry

    lax.fori_loop(1, peers, greet, 0)
    pl.semaphore_signal(
        barrier, inc=1, device_id=sibling, device_id_type=pl.DeviceIdType.MESH
    )
    locals_w = []
    for i, w in enumerate((gw, uw, dw)):
        c = pltpu.make_async_copy(w, W.at[i, core], w_loc.at[i])
        c.start()
        locals_w.append(c)
    pl.semaphore_wait(barrier, peers)

    def slot_rows(n):
        return pl.ds(pl.multiple_of(n * slots, slots), slots)

    def cols(z):
        return pl.ds(pl.multiple_of(z * chunk, chunk), chunk)

    def group_rows(z):
        return pl.ds(pl.multiple_of(z * per_group, per_group), per_group)

    def remote(src, dst, s, r, dev):
        c = pltpu.make_async_remote_copy(
            src_ref=src, dst_ref=dst, send_sem=s, recv_sem=r,
            device_id=dev, device_id_type=pl.DeviceIdType.MESH,
        )
        c.start()
        return c

    def out_to_owners(src, dst, i):
        pltpu.make_async_copy(
            src.at[slot_rows(me_e), cols(me_z)], dst.at[slot_rows(me)], a_loc.at[i]
        ).start()

        def body(k, carry):
            p = (me + k) % peers
            z, e = p // experts, p % experts
            remote(
                src.at[slot_rows(e), cols(z)], dst.at[slot_rows(me)],
                a_send.at[i], a_recv.at[i], at(z, e),
            )
            return carry

        lax.fori_loop(1, peers, body, 0)

    def out_to_sources(src, dst, i):
        pltpu.make_async_copy(
            src.at[slot_rows(me)], dst.at[slot_rows(me_e), cols(me_z)], a_loc.at[i]
        ).start()

        def body(k, carry):
            p = (me + k) % peers
            z, e = p // experts, p % experts
            remote(
                src.at[slot_rows(p)], dst.at[slot_rows(me_e), cols(me_z)],
                a_send.at[i], a_recv.at[i], at(z, e),
            )
            return carry

        lax.fori_loop(1, peers, body, 0)

    def take(sem, ref):
        pltpu.make_async_copy(ref, ref, sem).wait()

    some = pl.ds(0, (peers - 1) * slots)

    def arrived(i):
        take(a_recv.at[i], R.at[some])
        take(a_loc.at[i], R.at[pl.ds(0, slots)])

    out_to_owners(rows, R, 0)
    sent_w = [
        remote(w, W.at[i, core], w_send.at[i], w_recv.at[i], sibling)
        for i, w in enumerate((gw, uw, dw))
    ]

    step = min(256, all_rows)
    steps = all_rows // step

    def row_loop(fn):
        def body(j, carry):
            fn(pl.ds(pl.multiple_of(j * step, step), step))
            return carry

        lax.fori_loop(0, steps, body, 0)

    def scatter_sums(src, dst, i):
        for k in range(planes - 1, 0, -1):
            z = (me_z + k) % planes
            remote(
                src.at[group_rows(z)], dst.at[k - 1],
                p_send.at[i], p_recv.at[i], at(z, me_e),
            )

    def gather_rows(buf, i):
        for k in range(planes - 1, 0, -1):
            z = (me_z + k) % planes
            remote(
                buf.at[group_rows(me_z)], buf.at[group_rows(me_z)],
                h_send.at[i], h_recv.at[i], at(z, me_e),
            )

    def total(part, i, src, own):
        take(p_recv.at[i], part)
        for k in range(planes - 1):
            own = own + part[k].astype(F32)
        return own

    def weight(i):
        return W[i].reshape(chunk, ff)

    keep = pl.ds(pl.multiple_of(core * half, half), half)
    give = pl.ds(pl.multiple_of((1 - core) * half, half), half)

    arrived(0)
    for i in range(2):
        locals_w[i].wait()
        sent_w[i].wait_recv()

        def partial(rs, i=i):
            PS[i, rs, :] = dot(R[rs, :], weight(i), NN).astype(BF16)

        row_loop(partial)
        scatter_sums(PS.at[i], PR.at[i], i)
    x_rows = remote(R.at[:, give], RX, x_send.at[0], x_recv.at[0], sibling)
    mine = group_rows(me_z)
    gate_own = dot(R[mine, :], weight(0), NN)
    up_own = dot(R[mine, :], weight(1), NN)
    gate_pre = total(PR.at[0], 0, PS, gate_own)
    up_pre = total(PR.at[1], 1, PS, up_own)
    sigma = jax.nn.sigmoid(gate_pre)
    active = gate_pre * sigma
    H[mine, :] = (active * up_pre).astype(BF16)
    gather_rows(H, 0)
    locals_w[2].wait()
    sent_w[2].wait_recv()
    some_groups = pl.ds(0, (planes - 1) * per_group)
    take(h_recv.at[0], H.at[some_groups])

    def expert_out(rs):
        EO[rs, :] = dot(H[rs, :], weight(2), NT).astype(BF16)

    row_loop(expert_out)
    out_to_sources(EO, RET, 1)
    x_hidden = remote(H, HX, x_send.at[1], x_recv.at[1], sibling)
    arrived(1)
    for z in range(planes):
        piece = slice(z * chunk, (z + 1) * chunk)
        combined = dot(
            amat[...], RET[:, piece].astype(F32), NN, lax.Precision.HIGHEST
        )
        SG[:, piece] = (
            wcol[...] * (combined - tgt[:, piece].astype(F32))
        ).astype(BF16)
    out_to_owners(SG, G, 2)
    arrived(2)

    def hidden_partial(rs):
        HS[rs, :] = dot(G[rs, :], weight(2), NN).astype(BF16)

    row_loop(hidden_partial)
    scatter_sums(HS, HR, 2)
    x_grad = remote(G.at[:, give], GX, x_send.at[2], x_recv.at[2], sibling)
    own = dot(G[mine, :], weight(2), NN)
    hidden_grad = total(HR, 2, HS, own)
    GU[0, mine, :] = (
        hidden_grad * up_pre * sigma * (1.0 + gate_pre * (1.0 - sigma))
    ).astype(BF16)
    gather_rows(GU.at[0], 1)
    GU[1, mine, :] = (hidden_grad * active).astype(BF16)
    gather_rows(GU.at[1], 2)
    x_hidden.wait_recv()
    x_grad.wait_recv()
    x_rows.wait_recv()
    dg_out[...] = (dot(G[:, keep], H[...], TN) + dot(GX[...], HX[...], TN)) * factor
    take(h_recv.at[1], GU.at[0, some_groups])
    x_gate = remote(GU.at[0], GUX.at[0], x_send.at[3], x_recv.at[3], sibling)
    take(h_recv.at[2], GU.at[1, some_groups])

    def row_grad(rs):
        RG[rs, :] = (
            dot(GU[0, rs, :], weight(0), NT) + dot(GU[1, rs, :], weight(1), NT)
        ).astype(BF16)

    row_loop(row_grad)
    out_to_sources(RG, CB, 3)
    x_up = remote(GU.at[1], GUX.at[1], x_send.at[4], x_recv.at[4], sibling)
    x_gate.wait_recv()
    gg_out[...] = (
        dot(R[:, keep], GU[0], TN) + dot(RX[...], GUX[0], TN)
    ) * factor
    x_up.wait_recv()
    ug_out[...] = (
        dot(R[:, keep], GU[1], TN) + dot(RX[...], GUX[1], TN)
    ) * factor
    arrived(3)
    cb_out[...] = CB[...]

    for c in sent_w + [x_rows, x_hidden, x_grad, x_gate, x_up]:
        c.wait_send()
    for i in range(4):
        take(a_send.at[i], R.at[some])
    for i in range(2):
        take(p_send.at[i], PR.at[i])
    take(p_send.at[2], HR)
    for i in range(3):
        take(h_send.at[i], H.at[some_groups])


def on_device(
    tokens, target, route_index, route_count, route_gate, gate_weight, up_weight, down_weight
):
    groups = lax.axis_size("dp")
    experts = lax.axis_size("expert")
    planes = groups // CORES
    local_index = route_index[0, :, 0, :]
    live_count = route_count[0, :, 0]
    slots = local_index.shape[1]
    width = tokens.shape[1]
    half, _, ff = gate_weight.shape
    chunk = CORES * half
    usable = jnp.arange(slots, dtype=jnp.int32)[None, :] < live_count[:, None]
    slot_weight = jnp.where(usable, route_gate[0, :, 0, :], 0.0).reshape(-1)
    index = local_index.reshape(-1)
    rows = jnp.where(usable.reshape(-1)[:, None], tokens[index], jnp.zeros((), tokens.dtype))
    tgt = target[index]
    same = index[:, None] == index[None, :]
    amat = jnp.where(same, slot_weight[None, :], 0.0)
    picked = experts * slots
    all_rows = planes * picked
    vmem = pl.BlockSpec(memory_space=pltpu.VMEM)
    dma = pltpu.SemaphoreType.DMA
    came_back, gate_gradient, up_gradient, down_gradient = pl.pallas_call(
        functools.partial(
            kernel, planes, experts, slots, (groups * experts * slots) ** (-0.5)
        ),
        out_shape=(
            jax.ShapeDtypeStruct((picked, width), BF16),
            jax.ShapeDtypeStruct((half, ff), F32),
            jax.ShapeDtypeStruct((half, ff), F32),
            jax.ShapeDtypeStruct((half, ff), F32),
        ),
        in_specs=[vmem] * 7,
        out_specs=(vmem,) * 4,
        scratch_shapes=[
            pltpu.VMEM((3, CORES, half, ff), BF16),
            pltpu.VMEM((all_rows, chunk), BF16),
            pltpu.VMEM((all_rows, chunk), BF16),
            pltpu.VMEM((picked, width), BF16),
            pltpu.VMEM((picked, width), BF16),
            pltpu.VMEM((all_rows, chunk), BF16),
            pltpu.VMEM((all_rows, chunk), BF16),
            pltpu.VMEM((picked, width), BF16),
            pltpu.VMEM((2, all_rows, ff), BF16),
            pltpu.VMEM((2, planes - 1, picked, ff), BF16),
            pltpu.VMEM((all_rows, ff), BF16),
            pltpu.VMEM((planes - 1, picked, ff), BF16),
            pltpu.VMEM((all_rows, ff), BF16),
            pltpu.VMEM((2, all_rows, ff), BF16),
            pltpu.VMEM((all_rows, half), BF16),
            pltpu.VMEM((all_rows, half), BF16),
            pltpu.VMEM((all_rows, ff), BF16),
            pltpu.VMEM((2, all_rows, ff), BF16),
            dma((3,)), dma((3,)), dma((3,)),
            dma((4,)), dma((4,)), dma((4,)),
            dma((3,)), dma((3,)),
            dma((3,)), dma((3,)),
            dma((5,)), dma((5,)),
        ],
        compiler_params=pltpu.CompilerParams(
            collective_id=0, has_side_effects=True, vmem_limit_bytes=66000000
        ),
        name="routed_layer",
    )(
        rows, tgt, amat, slot_weight[:, None],
        gate_weight.reshape(half, ff), up_weight.reshape(half, ff),
        down_weight.reshape(half, ff),
    )
    spread = (
        jnp.arange(tokens.shape[0], dtype=jnp.int32)[:, None] == index[None, :]
    ).astype(BF16)
    token_grad = dot(spread, came_back, NN).astype(BF16)
    return (
        token_grad,
        gate_gradient.reshape(half, 1, ff),
        up_gradient.reshape(half, 1, ff),
        down_gradient.reshape(half, 1, ff),
    )


def solution(mesh):
    return jax.shard_map(
        on_device,
        mesh=mesh,
        in_specs=(
            P(("dp", "expert"), None),
            P(("dp", "expert"), None),
            P("dp", None, "expert", None),
            P("dp", None, "expert"),
            P("dp", None, "expert", None),
            P("dp", "expert", None),
            P("dp", "expert", None),
            P("dp", "expert", None),
        ),
        out_specs=(
            P(("dp", "expert"), None),
            P("dp", "expert", None),
            P("dp", "expert", None),
            P("dp", "expert", None),
        ),
        check_vma=False,
    )
```

```python
import functools

import jax
import jax.numpy as jnp
from jax import lax
from jax.experimental import pallas as pl
from jax.experimental.pallas import tpu as pltpu
from jax.sharding import PartitionSpec as P

F32 = jnp.float32
BF16 = jnp.bfloat16
VMEM_LIMIT = 67000000
CORES = 2


def dot(a, b, dims, precision=None):
    return lax.dot_general(
        a, b, (dims, ((), ())), preferred_element_type=F32, precision=precision
    )


NN = ((1,), (0,))
NT = ((1,), (1,))
TN = ((0,), (0,))


def kernel(
    planes, experts, slots, factor,
    index, count, gate, tokens, target, gw, uw, dw,
    cb_out, hot_out, gg_out, ug_out, dg_out,
    TOK, TGT, ROWS, TROWS, W, R, EO, RET, SG, G, RG, CB, PS, PR, H, GU, RX, GX, HX, GUX,
    t_loc, g_loc, w_loc, w_send, w_recv, a_loc, a_send, a_recv, p_send, p_recv,
    h_send, h_recv, x_send, x_recv,
):
    dp = lax.axis_index("dp")
    me_e = lax.axis_index("expert")
    me_z = dp // CORES
    core = dp % CORES
    peers = planes * experts
    per_group = experts * slots
    half = gw.shape[0]
    chunk = CORES * half
    ff = gw.shape[1]
    me = me_z * experts + me_e
    sibling = {"dp": me_z * CORES + (1 - core), "expert": me_e}
    order = sorted(range(1, planes), key=lambda k: -min(k, planes - k))

    def at(z, e):
        return {"dp": z * CORES + core, "expert": e}

    def plane(k):
        return (me_z + k) % planes

    def slot_rows(n):
        return pl.ds(pl.multiple_of(n * slots, slots), slots)

    def cols(z):
        return pl.ds(pl.multiple_of(z * chunk, chunk), chunk)

    def group_rows(z):
        return pl.ds(pl.multiple_of(z * per_group, per_group), per_group)

    barrier = pltpu.get_barrier_semaphore()

    def greet(k, carry):
        p = (me + k) % peers
        pl.semaphore_signal(
            barrier, inc=1, device_id=at(p // experts, p % experts),
            device_id_type=pl.DeviceIdType.MESH,
        )
        return carry

    lax.fori_loop(1, peers, greet, 0)
    pl.semaphore_signal(
        barrier, inc=1, device_id=sibling, device_id_type=pl.DeviceIdType.MESH
    )
    tok_copies = {}
    for k in order + [0]:
        z = plane(k)
        tok_copies[k] = pltpu.make_async_copy(
            tokens.at[:, cols(z)], TOK.at[:, cols(z)], t_loc.at[k]
        )
        tok_copies[k].start()
    locals_w = []
    for i, w in enumerate((gw, uw, dw)):
        c = pltpu.make_async_copy(w, W.at[i, core], w_loc.at[i])
        c.start()
        locals_w.append(c)
    tgt_copy = pltpu.make_async_copy(target, TGT, g_loc)
    tgt_copy.start()

    lane = lax.broadcasted_iota(jnp.int32, (slots, slots), 1)
    own_lane = lane == lax.broadcasted_iota(jnp.int32, (slots, slots), 0)
    slot_id = lax.broadcasted_iota(jnp.int32, (slots, 1), 0)
    names, weights = [], []
    for e in range(experts):
        live = slot_id < jnp.broadcast_to(count[0:1, e : e + 1], (slots, 1))
        ids = jnp.broadcast_to(index[0, e], (slots, slots))
        ids = jnp.sum(jnp.where(own_lane, ids, 0), axis=1, keepdims=True)
        names.append(jnp.where(live, ids, -1))
        g = jnp.broadcast_to(gate[0, e], (slots, slots))
        g = jnp.sum(jnp.where(own_lane, g, 0.0), axis=1, keepdims=True)
        weights.append(jnp.where(live, g, 0.0))
    names = jnp.concatenate(names, axis=0)
    wcol = jnp.concatenate(weights, axis=0)
    hot = (
        names == lax.broadcasted_iota(jnp.int32, (per_group, TOK.shape[0]), 1)
    ).astype(F32).astype(BF16)
    hot_out[...] = hot

    def remote(src, dst, s, r, dev):
        c = pltpu.make_async_remote_copy(
            src_ref=src, dst_ref=dst, send_sem=s, recv_sem=r,
            device_id=dev, device_id_type=pl.DeviceIdType.MESH,
        )
        c.start()
        return c

    def to_plane(i, k, source, land):
        z = plane(k)
        first = 0
        if k == 0:
            pltpu.make_async_copy(source(z, me_e), land, a_loc.at[i]).start()
            first = 1

        def send(j, carry):
            e = (me_e + j) % experts
            remote(source(z, e), land, a_send.at[i], a_recv.at[i, me_z], at(z, e))
            return carry

        lax.fori_loop(first, experts, send, 0)

    def owners(src, dst, i, k):
        to_plane(i, k, lambda z, e: src.at[slot_rows(e), cols(z)], dst.at[slot_rows(me)])

    def sources(src, dst, i, k):
        to_plane(
            i, k, lambda z, e: src.at[slot_rows(z * experts + e)],
            dst.at[slot_rows(me_e), cols(me_z)],
        )

    def take(sem, ref):
        pltpu.make_async_copy(ref, ref, sem).wait()

    def arrived(i, k):
        if k == 0:
            take(a_recv.at[i, me_z], R.at[pl.ds(0, (experts - 1) * slots)])
            take(a_loc.at[i], R.at[pl.ds(0, slots)])
        else:
            take(a_recv.at[i, plane(k)], R.at[pl.ds(0, per_group)])

    def weight(i):
        return W[i].reshape(chunk, ff)

    pl.semaphore_wait(barrier, peers)
    for k in order + [0]:
        z = plane(k)
        tok_copies[k].wait()
        ROWS[:, cols(z)] = dot(hot, TOK[:, cols(z)], NN).astype(BF16)
        owners(ROWS, R, 0, k)
    sent_w = [
        remote(w, W.at[i, core], w_send.at[i], w_recv.at[i], sibling)
        for i, w in enumerate((gw, uw, dw))
    ]

    def send_sum(i, k):
        remote(
            PS.at[i, group_rows(plane(k))], PR.at[i, k - 1],
            p_send.at[i], p_recv.at[i, k - 1], at(plane(k), me_e),
        )

    def spread(buf, i):
        mine = buf.at[group_rows(me_z)]
        for k in order:
            remote(mine, mine, h_send.at[i], h_recv.at[i, me_z], at(plane(k), me_e))

    def total(i, own):
        for k in order:
            take(p_recv.at[i, k - 1], PR.at[i, k - 1])
            own = own + PR[i, k - 1].astype(F32)
        return own

    keep = pl.ds(pl.multiple_of(core * half, half), half)
    give = pl.ds(pl.multiple_of((1 - core) * half, half), half)
    mine = group_rows(me_z)

    for i in range(2):
        locals_w[i].wait()
        sent_w[i].wait_recv()
    for k in order:
        z = plane(k)
        arrived(0, k)
        for i in range(2):
            PS[i, group_rows(z), :] = dot(R[group_rows(z), :], weight(i), NN).astype(BF16)
            send_sum(i, k)
    arrived(0, 0)
    gate_own = dot(R[mine, :], weight(0), NN)
    up_own = dot(R[mine, :], weight(1), NN)
    x_rows = remote(R.at[:, give], RX, x_send.at[0], x_recv.at[0], sibling)
    tgt_copy.wait()
    for z in range(planes):
        piece = slice(z * chunk, (z + 1) * chunk)
        TROWS[:, piece] = dot(hot, TGT[:, piece], NN)
    same = dot(hot, hot, NT).astype(BF16)
    gate_pre = total(0, gate_own)
    up_pre = total(1, up_own)
    sigma = jax.nn.sigmoid(gate_pre)
    active = gate_pre * sigma
    H[mine, :] = (active * up_pre).astype(BF16)
    spread(H, 0)
    locals_w[2].wait()
    sent_w[2].wait_recv()
    some_groups = pl.ds(0, (planes - 1) * per_group)

    for k in [0] + order:
        z = plane(k)
        if k:
            take(h_recv.at[0, z], H.at[group_rows(z)])
        EO[group_rows(z), :] = dot(H[group_rows(z), :], weight(2), NT).astype(BF16)
        sources(EO, RET, 1, k)
    x_hidden = remote(H, HX, x_send.at[1], x_recv.at[1], sibling)
    for k in order + [0]:
        z = plane(k)
        arrived(1, k)
        part = wcol * RET[:, cols(z)].astype(F32)
        combined = -TROWS[:, cols(z)]
        for _ in range(3):
            top = part.astype(BF16)
            combined = combined + dot(same, top, NN)
            part = part - top.astype(F32)
        SG[:, cols(z)] = (wcol * combined).astype(BF16)
        owners(SG, G, 2, k)

    for k in order:
        z = plane(k)
        arrived(2, k)
        PS[2, group_rows(z), :] = dot(G[group_rows(z), :], weight(2), NN).astype(BF16)
        send_sum(2, k)
    arrived(2, 0)
    own = dot(G[mine, :], weight(2), NN)
    x_grad = remote(G.at[:, give], GX, x_send.at[2], x_recv.at[2], sibling)
    x_hidden.wait_recv()
    x_grad.wait_recv()
    dg_out[...] = (dot(G[:, keep], H[...], TN) + dot(GX[...], HX[...], TN)) * factor
    hidden_grad = total(2, own)
    GU[0, mine, :] = (
        hidden_grad * up_pre * sigma * (1.0 + gate_pre * (1.0 - sigma))
    ).astype(BF16)
    spread(GU.at[0], 1)
    GU[1, mine, :] = (hidden_grad * active).astype(BF16)
    spread(GU.at[1], 2)

    for k in [0] + order:
        z = plane(k)
        if k:
            take(h_recv.at[1, z], H.at[group_rows(z)])
            take(h_recv.at[2, z], H.at[group_rows(z)])
        RG[group_rows(z), :] = (
            dot(GU[0, group_rows(z), :], weight(0), NT)
            + dot(GU[1, group_rows(z), :], weight(1), NT)
        ).astype(BF16)
        sources(RG, CB, 3, k)
    x_gate = remote(GU.at[0], GUX.at[0], x_send.at[3], x_recv.at[3], sibling)
    x_up = remote(GU.at[1], GUX.at[1], x_send.at[4], x_recv.at[4], sibling)
    x_rows.wait_recv()
    x_gate.wait_recv()
    gg_out[...] = (
        dot(R[:, keep], GU[0], TN) + dot(RX[...], GUX[0], TN)
    ) * factor
    x_up.wait_recv()
    ug_out[...] = (
        dot(R[:, keep], GU[1], TN) + dot(RX[...], GUX[1], TN)
    ) * factor
    for k in order + [0]:
        arrived(3, k)
    cb_out[...] = CB[...]

    for c in sent_w + [x_rows, x_hidden, x_grad, x_gate, x_up]:
        c.wait_send()
    for i in range(4):
        take(a_send.at[i], R.at[pl.ds(0, (peers - 1) * slots)])
    for i in range(3):
        take(p_send.at[i], PR.at[i])
        take(h_send.at[i], H.at[some_groups])


def finish(hot, cb, gg, ug, dg, tg_out, gg_out, ug_out, dg_out):
    tg_out[...] = dot(hot[...], cb[...], TN).astype(BF16)
    gg_out[:, 0, :] = gg[...]
    ug_out[:, 0, :] = ug[...]
    dg_out[:, 0, :] = dg[...]


def on_device(
    tokens, target, route_index, route_count, route_gate, gate_weight, up_weight, down_weight
):
    groups = lax.axis_size("dp")
    experts = lax.axis_size("expert")
    planes = groups // CORES
    slots = route_index.shape[3]
    count, width = tokens.shape
    half, _, ff = gate_weight.shape
    chunk = CORES * half
    picked = experts * slots
    all_rows = planes * picked
    vmem = pl.BlockSpec(memory_space=pltpu.VMEM)
    anyw = pl.BlockSpec(memory_space=pl.ANY)
    dma = pltpu.SemaphoreType.DMA
    grad = jax.ShapeDtypeStruct((half, ff), F32)
    came_back, hot, gate_gradient, up_gradient, down_gradient = pl.pallas_call(
        functools.partial(
            kernel, planes, experts, slots, (groups * experts * slots) ** (-0.5)
        ),
        out_shape=(
            jax.ShapeDtypeStruct((picked, width), BF16),
            jax.ShapeDtypeStruct((picked, count), BF16),
            grad, grad, grad,
        ),
        in_specs=[vmem] * 3 + [anyw] * 5,
        out_specs=(vmem,) * 5,
        scratch_shapes=[
            pltpu.VMEM((count, width), BF16),
            pltpu.VMEM((count, width), BF16),
            pltpu.VMEM((picked, width), BF16),
            pltpu.VMEM((picked, width), F32),
            pltpu.VMEM((3, CORES, half, ff), BF16),
            pltpu.VMEM((all_rows, chunk), BF16),
            pltpu.VMEM((all_rows, chunk), BF16),
            pltpu.VMEM((picked, width), BF16),
            pltpu.VMEM((picked, width), BF16),
            pltpu.VMEM((all_rows, chunk), BF16),
            pltpu.VMEM((all_rows, chunk), BF16),
            pltpu.VMEM((picked, width), BF16),
            pltpu.VMEM((3, all_rows, ff), BF16),
            pltpu.VMEM((3, planes - 1, picked, ff), BF16),
            pltpu.VMEM((all_rows, ff), BF16),
            pltpu.VMEM((2, all_rows, ff), BF16),
            pltpu.VMEM((all_rows, half), BF16),
            pltpu.VMEM((all_rows, half), BF16),
            pltpu.VMEM((all_rows, ff), BF16),
            pltpu.VMEM((2, all_rows, ff), BF16),
            dma((planes,)), dma,
            dma((3,)), dma((3,)), dma((3,)),
            dma((4,)), dma((4,)), dma((4, planes)),
            dma((3,)), dma((3, planes)),
            dma((3,)), dma((3, planes)),
            dma((5,)), dma((5,)),
        ],
        compiler_params=pltpu.CompilerParams(
            collective_id=0, has_side_effects=True, vmem_limit_bytes=VMEM_LIMIT
        ),
        name="routed_layer",
    )(
        route_index, route_count.reshape(1, experts), route_gate, tokens, target,
        gate_weight.reshape(half, ff), up_weight.reshape(half, ff),
        down_weight.reshape(half, ff),
    )
    steps = 2
    part = pl.BlockSpec((half // steps, ff), lambda i: (i, 0))
    part_out = pl.BlockSpec((half // steps, 1, ff), lambda i: (i, 0, 0))
    grad = jax.ShapeDtypeStruct((half, 1, ff), F32)
    return tuple(pl.pallas_call(
        finish,
        grid=(steps,),
        out_shape=(jax.ShapeDtypeStruct((count, width), BF16), grad, grad, grad),
        in_specs=[
            pl.BlockSpec((picked, count // steps), lambda i: (0, i)),
            pl.BlockSpec((picked, width), lambda i: (0, 0)),
            part, part, part,
        ],
        out_specs=(
            pl.BlockSpec((count // steps, width), lambda i: (i, 0)),
            part_out, part_out, part_out,
        ),
        compiler_params=pltpu.CompilerParams(vmem_limit_bytes=32000000),
        name="finish",
    )(hot, came_back, gate_gradient, up_gradient, down_gradient))


def solution(mesh):
    return jax.shard_map(
        on_device,
        mesh=mesh,
        in_specs=(
            P(("dp", "expert"), None),
            P(("dp", "expert"), None),
            P("dp", None, "expert", None),
            P("dp", None, "expert"),
            P("dp", None, "expert", None),
            P("dp", "expert", None),
            P("dp", "expert", None),
            P("dp", "expert", None),
        ),
        out_specs=(
            P(("dp", "expert"), None),
            P("dp", "expert", None),
            P("dp", "expert", None),
            P("dp", "expert", None),
        ),
        check_vma=False,
    )
```

```python
import functools

import jax
import jax.numpy as jnp
from jax import lax
from jax.experimental import pallas as pl
from jax.experimental.pallas import tpu as pltpu
from jax.sharding import PartitionSpec as P

F32 = jnp.float32
BF16 = jnp.bfloat16
VMEM_LIMIT = 67000000
CORES = 2


def dot(a, b, dims, precision=None):
    return lax.dot_general(
        a, b, (dims, ((), ())), preferred_element_type=F32, precision=precision
    )


NN = ((1,), (0,))
NT = ((1,), (1,))
TN = ((0,), (0,))


def kernel(
    planes, experts, slots, factor,
    index, count, gate, tokens, target, gw, uw, dw,
    cb_out, hot_out, gg_out, ug_out, dg_out,
    TOK, TGT, ROWS, TROWS, W, R, EO, RET, SG, G, RG, CB, PS, PR, H, GU, RX, GX, HX, GUX,
    t_loc, g_loc, w_loc, w_send, w_recv, a_loc, a_send, a_recv, p_send, p_recv,
    h_send, h_recv, x_send, x_recv, GRADS, o_loc,
):
    dp = lax.axis_index("dp")
    me_e = lax.axis_index("expert")
    me_z = dp // CORES
    core = dp % CORES
    peers = planes * experts
    per_group = experts * slots
    half = gw.shape[0]
    chunk = CORES * half
    ff = gw.shape[1]
    me = me_z * experts + me_e
    sibling = {"dp": me_z * CORES + (1 - core), "expert": me_e}
    order = sorted(range(1, planes), key=lambda k: -min(k, planes - k))

    def at(z, e):
        return {"dp": z * CORES + core, "expert": e}

    def plane(k):
        return (me_z + k) % planes

    def slot_rows(n):
        return pl.ds(pl.multiple_of(n * slots, slots), slots)

    def cols(z):
        return pl.ds(pl.multiple_of(z * chunk, chunk), chunk)

    def group_rows(z):
        return pl.ds(pl.multiple_of(z * per_group, per_group), per_group)

    barrier = pltpu.get_barrier_semaphore()

    def greet(k, carry):
        p = (me + k) % peers
        pl.semaphore_signal(
            barrier, inc=1, device_id=at(p // experts, p % experts),
            device_id_type=pl.DeviceIdType.MESH,
        )
        return carry

    lax.fori_loop(1, peers, greet, 0)
    pl.semaphore_signal(
        barrier, inc=1, device_id=sibling, device_id_type=pl.DeviceIdType.MESH
    )
    tok_copies = {}
    for k in order + [0]:
        z = plane(k)
        tok_copies[k] = pltpu.make_async_copy(
            tokens.at[:, cols(z)], TOK.at[:, cols(z)], t_loc.at[k]
        )
        tok_copies[k].start()
    locals_w = []
    for i, w in enumerate((gw, uw, dw)):
        c = pltpu.make_async_copy(w, W.at[i, core], w_loc.at[i])
        c.start()
        locals_w.append(c)
    tgt_copy = pltpu.make_async_copy(target, TGT, g_loc)
    tgt_copy.start()

    lane = lax.broadcasted_iota(jnp.int32, (slots, slots), 1)
    own_lane = lane == lax.broadcasted_iota(jnp.int32, (slots, slots), 0)
    slot_id = lax.broadcasted_iota(jnp.int32, (slots, 1), 0)
    names, weights = [], []
    for e in range(experts):
        live = slot_id < jnp.broadcast_to(count[0:1, e : e + 1], (slots, 1))
        ids = jnp.broadcast_to(index[0, e], (slots, slots))
        ids = jnp.sum(jnp.where(own_lane, ids, 0), axis=1, keepdims=True)
        names.append(jnp.where(live, ids, -1))
        g = jnp.broadcast_to(gate[0, e], (slots, slots))
        g = jnp.sum(jnp.where(own_lane, g, 0.0), axis=1, keepdims=True)
        weights.append(jnp.where(live, g, 0.0))
    names = jnp.concatenate(names, axis=0)
    wcol = jnp.concatenate(weights, axis=0)
    hot = (
        names == lax.broadcasted_iota(jnp.int32, (per_group, TOK.shape[0]), 1)
    ).astype(F32).astype(BF16)
    hot_out[...] = hot

    def remote(src, dst, s, r, dev):
        c = pltpu.make_async_remote_copy(
            src_ref=src, dst_ref=dst, send_sem=s, recv_sem=r,
            device_id=dev, device_id_type=pl.DeviceIdType.MESH,
        )
        c.start()
        return c

    def to_plane(i, z, source, land):
        here = z == me_z

        @pl.when(here)
        def _():
            pltpu.make_async_copy(source(me_z, me_e), land, a_loc.at[i]).start()

        first = jnp.where(here, 1, 0)

        def send(j, carry):
            e = (me_e + j) % experts
            remote(source(z, e), land, a_send.at[i], a_recv.at[i, me_z], at(z, e))
            return carry

        lax.fori_loop(first, experts, send, 0)

    def owners(src, dst, i, z):
        to_plane(i, z, lambda z, e: src.at[slot_rows(e), cols(z)], dst.at[slot_rows(me)])

    def sources(src, dst, i, z):
        to_plane(
            i, z, lambda z, e: src.at[slot_rows(z * experts + e)],
            dst.at[slot_rows(me_e), cols(me_z)],
        )

    def take(sem, ref):
        pltpu.make_async_copy(ref, ref, sem).wait()

    def arrived(i, k):
        if k == 0:
            take(a_recv.at[i, me_z], R.at[pl.ds(0, (experts - 1) * slots)])
            take(a_loc.at[i], R.at[pl.ds(0, slots)])
        else:
            take(a_recv.at[i, plane(k)], R.at[pl.ds(0, per_group)])

    outs = []

    def put(i, src, dst):
        c = pltpu.make_async_copy(src, dst, o_loc.at[i])
        c.start()
        outs.append(c)

    def weight(i):
        return W[i].reshape(chunk, ff)

    pl.semaphore_wait(barrier, peers)
    for k in order + [0]:
        z = plane(k)
        tok_copies[k].wait()
        ROWS[:, cols(z)] = dot(hot, TOK[:, cols(z)], NN).astype(BF16)
        owners(ROWS, R, 0, z)
    sent_w = [
        remote(w, W.at[i, core], w_send.at[i], w_recv.at[i], sibling)
        for i, w in enumerate((gw, uw, dw))
    ]

    def send_sum(i, k):
        remote(
            PS.at[i, group_rows(plane(k))], PR.at[i, k - 1],
            p_send.at[i], p_recv.at[i, k - 1], at(plane(k), me_e),
        )

    def pass_on(buf, i, s, way):
        to = me_z + way

        @pl.when(jnp.logical_and(to >= 0, to < planes))
        def _():
            rows_s = buf.at[group_rows(s)]
            remote(
                rows_s, rows_s, h_send.at[i, (way + 1) // 2, s], h_recv.at[i, s],
                at(to, me_e),
            )

    def spread(buf, i):
        for way in (1, -1):
            pass_on(buf, i, me_z, way)

    def along(bufs, first, fn):
        fn(me_z)
        for far in range(1, planes):
            for way in (1, -1):
                s = me_z - way * far

                @pl.when(jnp.logical_and(s >= 0, s < planes))
                def _():
                    for j, buf in enumerate(bufs):
                        take(h_recv.at[first + j, s], buf.at[group_rows(s)])
                        pass_on(buf, first + j, s, way)
                    fn(s)

    def spread_sent(buf, i):
        for s in range(planes):
            rows_s = buf.at[pl.ds(s * per_group, per_group)]

            @pl.when(jnp.logical_and(me_z > 0, me_z <= s))
            def _():
                take(h_send.at[i, 0, s], rows_s)

            @pl.when(jnp.logical_and(me_z < planes - 1, me_z >= s))
            def _():
                take(h_send.at[i, 1, s], rows_s)

    def total(i, own):
        for k in order:
            take(p_recv.at[i, k - 1], PR.at[i, k - 1])
            own = own + PR[i, k - 1].astype(F32)
        return own

    keep = pl.ds(pl.multiple_of(core * half, half), half)
    give = pl.ds(pl.multiple_of((1 - core) * half, half), half)
    mine = group_rows(me_z)

    for i in range(2):
        locals_w[i].wait()
        sent_w[i].wait_recv()
    for k in order:
        z = plane(k)
        arrived(0, k)
        for i in range(2):
            PS[i, group_rows(z), :] = dot(R[group_rows(z), :], weight(i), NN).astype(BF16)
            send_sum(i, k)
    arrived(0, 0)
    gate_own = dot(R[mine, :], weight(0), NN)
    up_own = dot(R[mine, :], weight(1), NN)
    x_rows = remote(R.at[:, give], RX, x_send.at[0], x_recv.at[0], sibling)
    tgt_copy.wait()
    for z in range(planes):
        piece = slice(z * chunk, (z + 1) * chunk)
        TROWS[:, piece] = dot(hot, TGT[:, piece], NN)
    same = dot(hot, hot, NT).astype(BF16)
    gate_pre = total(0, gate_own)
    up_pre = total(1, up_own)
    sigma = jax.nn.sigmoid(gate_pre)
    active = gate_pre * sigma
    H[mine, :] = (active * up_pre).astype(BF16)
    spread(H, 0)
    locals_w[2].wait()
    sent_w[2].wait_recv()

    def expert_out(z):
        EO[group_rows(z), :] = dot(H[group_rows(z), :], weight(2), NT).astype(BF16)
        sources(EO, RET, 1, z)

    along([H], 0, expert_out)
    x_hidden = remote(H, HX, x_send.at[1], x_recv.at[1], sibling)
    for k in order + [0]:
        z = plane(k)
        arrived(1, k)
        part = wcol * RET[:, cols(z)].astype(F32)
        combined = -TROWS[:, cols(z)]
        for _ in range(3):
            top = part.astype(BF16)
            combined = combined + dot(same, top, NN)
            part = part - top.astype(F32)
        SG[:, cols(z)] = (wcol * combined).astype(BF16)
        owners(SG, G, 2, z)

    for k in order:
        z = plane(k)
        arrived(2, k)
        PS[2, group_rows(z), :] = dot(G[group_rows(z), :], weight(2), NN).astype(BF16)
        send_sum(2, k)
    arrived(2, 0)
    own = dot(G[mine, :], weight(2), NN)
    x_grad = remote(G.at[:, give], GX, x_send.at[2], x_recv.at[2], sibling)
    x_hidden.wait_recv()
    x_grad.wait_recv()
    GRADS[2] = (dot(G[:, keep], H[...], TN) + dot(GX[...], HX[...], TN)) * factor
    put(2, GRADS.at[2], dg_out)
    hidden_grad = total(2, own)
    GU[0, mine, :] = (
        hidden_grad * up_pre * sigma * (1.0 + gate_pre * (1.0 - sigma))
    ).astype(BF16)
    spread(GU.at[0], 1)
    GU[1, mine, :] = (hidden_grad * active).astype(BF16)
    spread(GU.at[1], 2)

    def row_grad(z):
        RG[group_rows(z), :] = (
            dot(GU[0, group_rows(z), :], weight(0), NT)
            + dot(GU[1, group_rows(z), :], weight(1), NT)
        ).astype(BF16)
        sources(RG, CB, 3, z)

    along([GU.at[0], GU.at[1]], 1, row_grad)
    x_gate = remote(GU.at[0], GUX.at[0], x_send.at[3], x_recv.at[3], sibling)
    x_up = remote(GU.at[1], GUX.at[1], x_send.at[4], x_recv.at[4], sibling)
    x_rows.wait_recv()
    x_gate.wait_recv()
    GRADS[0] = (dot(R[:, keep], GU[0], TN) + dot(RX[...], GUX[0], TN)) * factor
    put(0, GRADS.at[0], gg_out)
    x_up.wait_recv()
    GRADS[1] = (dot(R[:, keep], GU[1], TN) + dot(RX[...], GUX[1], TN)) * factor
    put(1, GRADS.at[1], ug_out)
    for k in order + [0]:
        arrived(3, k)
    put(3, CB, cb_out)

    for c in sent_w + [x_rows, x_hidden, x_grad, x_gate, x_up]:
        c.wait_send()
    for i in range(4):
        take(a_send.at[i], R.at[pl.ds(0, (peers - 1) * slots)])
    for i in range(3):
        take(p_send.at[i], PR.at[i])
    for i, buf in enumerate((H, GU.at[0], GU.at[1])):
        spread_sent(buf, i)
    for c in outs:
        c.wait()


def finish(hot, cb, gg, ug, dg, tg_out, gg_out, ug_out, dg_out):
    tg_out[...] = dot(hot[...], cb[...], TN).astype(BF16)
    gg_out[:, 0, :] = gg[...]
    ug_out[:, 0, :] = ug[...]
    dg_out[:, 0, :] = dg[...]


def on_device(
    tokens, target, route_index, route_count, route_gate, gate_weight, up_weight, down_weight
):
    groups = lax.axis_size("dp")
    experts = lax.axis_size("expert")
    planes = groups // CORES
    slots = route_index.shape[3]
    count, width = tokens.shape
    half, _, ff = gate_weight.shape
    chunk = CORES * half
    picked = experts * slots
    all_rows = planes * picked
    vmem = pl.BlockSpec(memory_space=pltpu.VMEM)
    anyw = pl.BlockSpec(memory_space=pl.ANY)
    dma = pltpu.SemaphoreType.DMA
    grad = jax.ShapeDtypeStruct((half, ff), F32)
    came_back, hot, gate_gradient, up_gradient, down_gradient = pl.pallas_call(
        functools.partial(
            kernel, planes, experts, slots, (groups * experts * slots) ** (-0.5)
        ),
        out_shape=(
            jax.ShapeDtypeStruct((picked, width), BF16),
            jax.ShapeDtypeStruct((picked, count), BF16),
            grad, grad, grad,
        ),
        in_specs=[vmem] * 3 + [anyw] * 5,
        out_specs=(anyw, vmem) + (anyw,) * 3,
        scratch_shapes=[
            pltpu.VMEM((count, width), BF16),
            pltpu.VMEM((count, width), BF16),
            pltpu.VMEM((picked, width), BF16),
            pltpu.VMEM((picked, width), F32),
            pltpu.VMEM((3, CORES, half, ff), BF16),
            pltpu.VMEM((all_rows, chunk), BF16),
            pltpu.VMEM((all_rows, chunk), BF16),
            pltpu.VMEM((picked, width), BF16),
            pltpu.VMEM((picked, width), BF16),
            pltpu.VMEM((all_rows, chunk), BF16),
            pltpu.VMEM((all_rows, chunk), BF16),
            pltpu.VMEM((picked, width), BF16),
            pltpu.VMEM((3, all_rows, ff), BF16),
            pltpu.VMEM((3, planes - 1, picked, ff), BF16),
            pltpu.VMEM((all_rows, ff), BF16),
            pltpu.VMEM((2, all_rows, ff), BF16),
            pltpu.VMEM((all_rows, half), BF16),
            pltpu.VMEM((all_rows, half), BF16),
            pltpu.VMEM((all_rows, ff), BF16),
            pltpu.VMEM((2, all_rows, ff), BF16),
            dma((planes,)), dma,
            dma((3,)), dma((3,)), dma((3,)),
            dma((4,)), dma((4,)), dma((4, planes)),
            dma((3,)), dma((3, planes)),
            dma((3, 2, planes)), dma((3, planes)),
            dma((5,)), dma((5,)),
            pltpu.VMEM((3, half, ff), F32), dma((4,)),
        ],
        compiler_params=pltpu.CompilerParams(
            collective_id=0, has_side_effects=True, vmem_limit_bytes=VMEM_LIMIT
        ),
        name="routed_layer",
    )(
        route_index, route_count.reshape(1, experts), route_gate, tokens, target,
        gate_weight.reshape(half, ff), up_weight.reshape(half, ff),
        down_weight.reshape(half, ff),
    )
    steps = 2
    part = pl.BlockSpec((half // steps, ff), lambda i: (i, 0))
    part_out = pl.BlockSpec((half // steps, 1, ff), lambda i: (i, 0, 0))
    grad = jax.ShapeDtypeStruct((half, 1, ff), F32)
    return tuple(pl.pallas_call(
        finish,
        grid=(steps,),
        out_shape=(jax.ShapeDtypeStruct((count, width), BF16), grad, grad, grad),
        in_specs=[
            pl.BlockSpec((picked, count // steps), lambda i: (0, i)),
            pl.BlockSpec((picked, width), lambda i: (0, 0)),
            part, part, part,
        ],
        out_specs=(
            pl.BlockSpec((count // steps, width), lambda i: (i, 0)),
            part_out, part_out, part_out,
        ),
        compiler_params=pltpu.CompilerParams(vmem_limit_bytes=VMEM_LIMIT),
        name="finish",
    )(hot, came_back, gate_gradient, up_gradient, down_gradient))


def solution(mesh):
    return jax.shard_map(
        on_device,
        mesh=mesh,
        in_specs=(
            P(("dp", "expert"), None),
            P(("dp", "expert"), None),
            P("dp", None, "expert", None),
            P("dp", None, "expert"),
            P("dp", None, "expert", None),
            P("dp", "expert", None),
            P("dp", "expert", None),
            P("dp", "expert", None),
        ),
        out_specs=(
            P(("dp", "expert"), None),
            P("dp", "expert", None),
            P("dp", "expert", None),
            P("dp", "expert", None),
        ),
        check_vma=False,
    )
```

```python
import functools

import jax
import jax.numpy as jnp
from jax import lax
from jax.experimental import pallas as pl
from jax.experimental.pallas import tpu as pltpu
from jax.sharding import PartitionSpec as P

F32 = jnp.float32
BF16 = jnp.bfloat16
VMEM_LIMIT = 67000000
CORES = 2


def dot(a, b, dims, precision=None):
    return lax.dot_general(
        a, b, (dims, ((), ())), preferred_element_type=F32, precision=precision
    )


NN = ((1,), (0,))
NT = ((1,), (1,))
TN = ((0,), (0,))


def kernel(
    planes, experts, slots, factor,
    index, count, gate, tokens, target, gw, uw, dw,
    cb_out, hot_out, gg_out, ug_out, dg_out,
    TOK, TGT, ROWS, TROWS, W, R, EO, RET, SG, G, RG, CB, PS, PR, H, GU, RX, GX, HX, GUX,
    t_loc, g_loc, w_loc, w_send, w_recv, a_loc, a_send, a_recv, p_send, p_recv,
    h_send, h_recv, x_send, x_recv, GRADS, o_loc,
):
    dp = lax.axis_index("dp")
    me_e = lax.axis_index("expert")
    me_z = dp // CORES
    core = dp % CORES
    peers = planes * experts
    per_group = experts * slots
    half = gw.shape[0]
    chunk = CORES * half
    ff = gw.shape[1]
    me = me_z * experts + me_e
    sibling = {"dp": me_z * CORES + (1 - core), "expert": me_e}
    order = sorted(range(1, planes), key=lambda k: -min(k, planes - k))

    def at(z, e):
        return {"dp": z * CORES + core, "expert": e}

    def plane(k):
        return (me_z + k) % planes

    def slot_rows(n):
        return pl.ds(pl.multiple_of(n * slots, slots), slots)

    def cols(z):
        return pl.ds(pl.multiple_of(z * chunk, chunk), chunk)

    def group_rows(z):
        return pl.ds(pl.multiple_of(z * per_group, per_group), per_group)

    barrier = pltpu.get_barrier_semaphore()

    def greet(k, carry):
        p = (me + k) % peers
        pl.semaphore_signal(
            barrier, inc=1, device_id=at(p // experts, p % experts),
            device_id_type=pl.DeviceIdType.MESH,
        )
        return carry

    lax.fori_loop(1, peers, greet, 0)
    pl.semaphore_signal(
        barrier, inc=1, device_id=sibling, device_id_type=pl.DeviceIdType.MESH
    )
    tok_copies = {}
    for k in order + [0]:
        z = plane(k)
        tok_copies[k] = pltpu.make_async_copy(
            tokens.at[:, cols(z)], TOK.at[:, cols(z)], t_loc.at[k]
        )
        tok_copies[k].start()
    locals_w = []
    for i, w in enumerate((gw, uw, dw)):
        c = pltpu.make_async_copy(w, W.at[i, core], w_loc.at[i])
        c.start()
        locals_w.append(c)
    tgt_copy = pltpu.make_async_copy(target, TGT, g_loc)
    tgt_copy.start()

    lane = lax.broadcasted_iota(jnp.int32, (slots, slots), 1)
    own_lane = lane == lax.broadcasted_iota(jnp.int32, (slots, slots), 0)
    slot_id = lax.broadcasted_iota(jnp.int32, (slots, 1), 0)
    names, weights = [], []
    for e in range(experts):
        live = slot_id < jnp.broadcast_to(count[0:1, e : e + 1], (slots, 1))
        ids = jnp.broadcast_to(index[0, e], (slots, slots))
        ids = jnp.sum(jnp.where(own_lane, ids, 0), axis=1, keepdims=True)
        names.append(jnp.where(live, ids, -1))
        g = jnp.broadcast_to(gate[0, e], (slots, slots))
        g = jnp.sum(jnp.where(own_lane, g, 0.0), axis=1, keepdims=True)
        weights.append(jnp.where(live, g, 0.0))
    names = jnp.concatenate(names, axis=0)
    wcol = jnp.concatenate(weights, axis=0)
    hot = (
        names == lax.broadcasted_iota(jnp.int32, (per_group, TOK.shape[0]), 1)
    ).astype(F32).astype(BF16)
    hot_out[...] = hot

    def remote(src, dst, s, r, dev):
        c = pltpu.make_async_remote_copy(
            src_ref=src, dst_ref=dst, send_sem=s, recv_sem=r,
            device_id=dev, device_id_type=pl.DeviceIdType.MESH,
        )
        c.start()
        return c

    def to_plane(i, z, source, land):
        here = z == me_z

        @pl.when(here)
        def _():
            pltpu.make_async_copy(source(me_z, me_e), land, a_loc.at[i]).start()

        first = jnp.where(here, 1, 0)

        def send(j, carry):
            e = (me_e + j) % experts
            remote(source(z, e), land, a_send.at[i], a_recv.at[i, me_z], at(z, e))
            return carry

        lax.fori_loop(first, experts, send, 0)

    def owners(src, dst, i, z):
        to_plane(i, z, lambda z, e: src.at[slot_rows(e), cols(z)], dst.at[slot_rows(me)])

    def sources(src, dst, i, z):
        to_plane(
            i, z, lambda z, e: src.at[slot_rows(z * experts + e)],
            dst.at[slot_rows(me_e), cols(me_z)],
        )

    def take(sem, ref):
        pltpu.make_async_copy(ref, ref, sem).wait()

    def arrived(i, k):
        if k == 0:
            take(a_recv.at[i, me_z], R.at[pl.ds(0, (experts - 1) * slots)])
            take(a_loc.at[i], R.at[pl.ds(0, slots)])
        else:
            take(a_recv.at[i, plane(k)], R.at[pl.ds(0, per_group)])

    outs = []

    def put(i, src, dst):
        c = pltpu.make_async_copy(src, dst, o_loc.at[i])
        c.start()
        outs.append(c)

    def weight(i):
        return W[i].reshape(chunk, ff)

    pl.semaphore_wait(barrier, peers)
    for k in order + [0]:
        z = plane(k)
        tok_copies[k].wait()
        ROWS[:, cols(z)] = dot(hot, TOK[:, cols(z)], NN).astype(BF16)
        owners(ROWS, R, 0, z)
    sent_w = [
        remote(w, W.at[i, core], w_send.at[i], w_recv.at[i], sibling)
        for i, w in enumerate((gw, uw, dw))
    ]

    def send_sum(i, k):
        remote(
            PS.at[i, group_rows(plane(k))], PR.at[i, k - 1],
            p_send.at[i], p_recv.at[i, k - 1], at(plane(k), me_e),
        )

    def pass_on(buf, i, s, way):
        to = me_z + way

        @pl.when(jnp.logical_and(to >= 0, to < planes))
        def _():
            rows_s = buf.at[group_rows(s)]
            remote(
                rows_s, rows_s, h_send.at[i, (way + 1) // 2, s], h_recv.at[i, s],
                at(to, me_e),
            )

    def spread(buf, i):
        for way in (1, -1):
            pass_on(buf, i, me_z, way)

    def along(bufs, first, fn):
        fn(me_z)
        for far in range(1, planes):
            for way in (1, -1):
                s = me_z - way * far

                @pl.when(jnp.logical_and(s >= 0, s < planes))
                def _():
                    for j, buf in enumerate(bufs):
                        take(h_recv.at[first + j, s], buf.at[group_rows(s)])
                        pass_on(buf, first + j, s, way)
                    fn(s)

    def spread_sent(buf, i):
        for s in range(planes):
            rows_s = buf.at[pl.ds(s * per_group, per_group)]

            @pl.when(jnp.logical_and(me_z > 0, me_z <= s))
            def _():
                take(h_send.at[i, 0, s], rows_s)

            @pl.when(jnp.logical_and(me_z < planes - 1, me_z >= s))
            def _():
                take(h_send.at[i, 1, s], rows_s)

    def total(i, own):
        for k in order:
            take(p_recv.at[i, k - 1], PR.at[i, k - 1])
            own = own + PR[i, k - 1].astype(F32)
        return own

    keep = pl.ds(pl.multiple_of(core * half, half), half)
    give = pl.ds(pl.multiple_of((1 - core) * half, half), half)
    mine = group_rows(me_z)

    for i in range(2):
        locals_w[i].wait()
        sent_w[i].wait_recv()
    for k in order:
        z = plane(k)
        arrived(0, k)
        for i in range(2):
            PS[i, group_rows(z), :] = dot(R[group_rows(z), :], weight(i), NN).astype(BF16)
            send_sum(i, k)
    arrived(0, 0)
    gate_own = dot(R[mine, :], weight(0), NN)
    up_own = dot(R[mine, :], weight(1), NN)
    x_rows = remote(R.at[:, give], RX, x_send.at[0], x_recv.at[0], sibling)
    tgt_copy.wait()
    for z in range(planes):
        piece = slice(z * chunk, (z + 1) * chunk)
        TROWS[:, piece] = dot(hot, TGT[:, piece], NN)
    same = dot(hot, hot, NT).astype(BF16)
    gate_pre = total(0, gate_own)
    up_pre = total(1, up_own)
    sigma = jax.nn.sigmoid(gate_pre)
    active = gate_pre * sigma
    H[mine, :] = (active * up_pre).astype(BF16)
    spread(H, 0)
    locals_w[2].wait()
    sent_w[2].wait_recv()

    def expert_out(z):
        EO[group_rows(z), :] = dot(H[group_rows(z), :], weight(2), NT).astype(BF16)
        sources(EO, RET, 1, z)

    along([H], 0, expert_out)
    x_hidden = remote(H, HX, x_send.at[1], x_recv.at[1], sibling)
    for k in order + [0]:
        z = plane(k)
        arrived(1, k)
        part = wcol * RET[:, cols(z)].astype(F32)
        combined = -TROWS[:, cols(z)]
        for _ in range(3):
            top = part.astype(BF16)
            combined = combined + dot(same, top, NN)
            part = part - top.astype(F32)
        SG[:, cols(z)] = (wcol * combined).astype(BF16)
        owners(SG, G, 2, z)

    for k in order:
        z = plane(k)
        arrived(2, k)
        PS[2, group_rows(z), :] = dot(G[group_rows(z), :], weight(2), NN).astype(BF16)
        send_sum(2, k)
    arrived(2, 0)
    own = dot(G[mine, :], weight(2), NN)
    x_grad = remote(G.at[:, give], GX, x_send.at[2], x_recv.at[2], sibling)
    x_hidden.wait_recv()
    x_grad.wait_recv()
    GRADS[2] = (dot(G[:, keep], H[...], TN) + dot(GX[...], HX[...], TN)) * factor
    put(2, GRADS.at[2], dg_out)
    hidden_grad = total(2, own)
    GU[0, mine, :] = (
        hidden_grad * up_pre * sigma * (1.0 + gate_pre * (1.0 - sigma))
    ).astype(BF16)
    spread(GU.at[0], 1)
    GU[1, mine, :] = (hidden_grad * active).astype(BF16)
    spread(GU.at[1], 2)

    def row_grad(z):
        RG[group_rows(z), :] = (
            dot(GU[0, group_rows(z), :], weight(0), NT)
            + dot(GU[1, group_rows(z), :], weight(1), NT)
        ).astype(BF16)
        sources(RG, CB, 3, z)
        for i in range(2):
            remote(
                GU.at[i, group_rows(z)], GUX.at[i, group_rows(z)],
                x_send.at[3 + i], x_recv.at[3 + i], sibling,
            )

    along([GU.at[0], GU.at[1]], 1, row_grad)
    own_sums = [dot(R[:, keep], GU[i], TN) for i in range(2)]
    x_rows.wait_recv()
    for i, out in enumerate((gg_out, ug_out)):
        take(x_recv.at[3 + i], GUX.at[i])
        GRADS[i] = (own_sums[i] + dot(RX[...], GUX[i], TN)) * factor
        put(i, GRADS.at[i], out)
    for k in order + [0]:
        arrived(3, k)
    put(3, CB, cb_out)

    for c in sent_w + [x_rows, x_hidden, x_grad]:
        c.wait_send()
    for i in range(2):
        take(x_send.at[3 + i], GUX.at[i])
    for i in range(4):
        take(a_send.at[i], R.at[pl.ds(0, (peers - 1) * slots)])
    for i in range(3):
        take(p_send.at[i], PR.at[i])
    for i, buf in enumerate((H, GU.at[0], GU.at[1])):
        spread_sent(buf, i)
    for c in outs:
        c.wait()


def finish(hot, cb, gg, ug, dg, tg_out, gg_out, ug_out, dg_out):
    tg_out[...] = dot(hot[...], cb[...], TN).astype(BF16)
    gg_out[:, 0, :] = gg[...]
    ug_out[:, 0, :] = ug[...]
    dg_out[:, 0, :] = dg[...]


def on_device(
    tokens, target, route_index, route_count, route_gate, gate_weight, up_weight, down_weight
):
    groups = lax.axis_size("dp")
    experts = lax.axis_size("expert")
    planes = groups // CORES
    slots = route_index.shape[3]
    count, width = tokens.shape
    half, _, ff = gate_weight.shape
    chunk = CORES * half
    picked = experts * slots
    all_rows = planes * picked
    vmem = pl.BlockSpec(memory_space=pltpu.VMEM)
    anyw = pl.BlockSpec(memory_space=pl.ANY)
    dma = pltpu.SemaphoreType.DMA
    grad = jax.ShapeDtypeStruct((half, ff), F32)
    came_back, hot, gate_gradient, up_gradient, down_gradient = pl.pallas_call(
        functools.partial(
            kernel, planes, experts, slots, (groups * experts * slots) ** (-0.5)
        ),
        out_shape=(
            jax.ShapeDtypeStruct((picked, width), BF16),
            jax.ShapeDtypeStruct((picked, count), BF16),
            grad, grad, grad,
        ),
        in_specs=[vmem] * 3 + [anyw] * 5,
        out_specs=(anyw, vmem) + (anyw,) * 3,
        scratch_shapes=[
            pltpu.VMEM((count, width), BF16),
            pltpu.VMEM((count, width), BF16),
            pltpu.VMEM((picked, width), BF16),
            pltpu.VMEM((picked, width), F32),
            pltpu.VMEM((3, CORES, half, ff), BF16),
            pltpu.VMEM((all_rows, chunk), BF16),
            pltpu.VMEM((all_rows, chunk), BF16),
            pltpu.VMEM((picked, width), BF16),
            pltpu.VMEM((picked, width), BF16),
            pltpu.VMEM((all_rows, chunk), BF16),
            pltpu.VMEM((all_rows, chunk), BF16),
            pltpu.VMEM((picked, width), BF16),
            pltpu.VMEM((3, all_rows, ff), BF16),
            pltpu.VMEM((3, planes - 1, picked, ff), BF16),
            pltpu.VMEM((all_rows, ff), BF16),
            pltpu.VMEM((2, all_rows, ff), BF16),
            pltpu.VMEM((all_rows, half), BF16),
            pltpu.VMEM((all_rows, half), BF16),
            pltpu.VMEM((all_rows, ff), BF16),
            pltpu.VMEM((2, all_rows, ff), BF16),
            dma((planes,)), dma,
            dma((3,)), dma((3,)), dma((3,)),
            dma((4,)), dma((4,)), dma((4, planes)),
            dma((3,)), dma((3, planes)),
            dma((3, 2, planes)), dma((3, planes)),
            dma((5,)), dma((5,)),
            pltpu.VMEM((3, half, ff), F32), dma((4,)),
        ],
        compiler_params=pltpu.CompilerParams(
            collective_id=0, has_side_effects=True, vmem_limit_bytes=VMEM_LIMIT
        ),
        name="routed_layer",
    )(
        route_index, route_count.reshape(1, experts), route_gate, tokens, target,
        gate_weight.reshape(half, ff), up_weight.reshape(half, ff),
        down_weight.reshape(half, ff),
    )
    steps = 2
    part = pl.BlockSpec((half // steps, ff), lambda i: (i, 0))
    part_out = pl.BlockSpec((half // steps, 1, ff), lambda i: (i, 0, 0))
    grad = jax.ShapeDtypeStruct((half, 1, ff), F32)
    return tuple(pl.pallas_call(
        finish,
        grid=(steps,),
        out_shape=(jax.ShapeDtypeStruct((count, width), BF16), grad, grad, grad),
        in_specs=[
            pl.BlockSpec((picked, count // steps), lambda i: (0, i)),
            pl.BlockSpec((picked, width), lambda i: (0, 0)),
            part, part, part,
        ],
        out_specs=(
            pl.BlockSpec((count // steps, width), lambda i: (i, 0)),
            part_out, part_out, part_out,
        ),
        compiler_params=pltpu.CompilerParams(vmem_limit_bytes=VMEM_LIMIT),
        name="finish",
    )(hot, came_back, gate_gradient, up_gradient, down_gradient))


def solution(mesh):
    return jax.shard_map(
        on_device,
        mesh=mesh,
        in_specs=(
            P(("dp", "expert"), None),
            P(("dp", "expert"), None),
            P("dp", None, "expert", None),
            P("dp", None, "expert"),
            P("dp", None, "expert", None),
            P("dp", "expert", None),
            P("dp", "expert", None),
            P("dp", "expert", None),
        ),
        out_specs=(
            P(("dp", "expert"), None),
            P("dp", "expert", None),
            P("dp", "expert", None),
            P("dp", "expert", None),
        ),
        check_vma=False,
    )
```
